32 devices in a mesh: seq: 4 (over z), tp: 4 (over x, core), dp: 2 (over y).
Axes of the slice: x: 2, y: 2, z: 4, core: 2. Of those that a mesh axis runs over, the one named last changes fastest.
Arguments:
- queries: bfloat16 [2, 512, 4096], P('dp', 'seq', 'tp'), may hold values from -0.5 to 0.5
- keys: bfloat16 [2, 512, 4096], P('dp', 'seq', 'tp'), may hold values from -0.25 to 0.25
- values: bfloat16 [2, 512, 4096], P('dp', 'seq', 'tp'), may hold values from -19 to 19
- out_gain: float32 [4096], P('tp'), may hold values from 0.1 to 1.9
- grad_out: bfloat16 [2, 512, 4096], P('dp', 'seq', 'tp'), may hold values from -12 to 12
Outputs:
- normed: bfloat16 [2, 512, 4096], P('dp', 'seq', 'tp')
- query_gradient: bfloat16 [2, 512, 4096], P('dp', 'seq', 'tp')
- grad_keys: bfloat16 [2, 512, 4096], P('dp', 'seq', 'tp')
- value_gradient: bfloat16 [2, 512, 4096], P('dp', 'seq', 'tp')
- gain_grad: float32 [4096], P('tp')
The draws below stay inside these ranges and needn't reach their ends.
All inputs are finite; a program needn't handle non-finite values.
Results may differ from the reference program's by a relative error of at most 0.005.
Values sent between devices are 32-bit elements; how exact they have to be, the bound alone decides.
A program may use at most 64 MiB of HBM per device.

```python
import jax
import jax.numpy as jnp
from jax import lax

HEADS = 32
HD = 128
HID = 4096
BLOCK = 128
TOKENS = 512
SEQS = 2


def rough_base(base_key, shape, bound):
    return jnp.clip(jax.random.normal(base_key, shape, jnp.float32), -bound, bound)


def draw_values(key, part):
    own_key = jax.random.fold_in(key, 17)
    base_key, jitter_key = jax.random.split(own_key, 2)
    base = rough_base(base_key, (SEQS, TOKENS, HEADS, HD), 6.0)
    jitter = jax.random.uniform(jitter_key, (HEADS,), jnp.float32)
    spread = 10.0 ** (0.5 * (jnp.arange(HEADS).astype(jnp.float32) + jitter) / HEADS)
    return (base * spread[None, None, :, None]).reshape(SEQS, TOKENS, HID).astype(jnp.bfloat16)


def draw_grad_out(key, part):
    own_key = jax.random.fold_in(key, 29)
    base_key, jitter_key = jax.random.split(own_key, 2)
    base = rough_base(base_key, (SEQS, TOKENS, HID), 4.0)
    jitter = jax.random.uniform(jitter_key, (SEQS, TOKENS), jnp.float32)
    exponent = 0.7 * jnp.arange(TOKENS).astype(jnp.float32)[None, :] / TOKENS + 0.3 * jitter
    return (base * (0.3 * 10.0 ** exponent)[:, :, None]).astype(jnp.bfloat16)


def block_levels(rng, extent, shards, smallest, high):
    gain = 1.0
    for position, parts in shards:
        steps = jax.random.uniform(jax.random.fold_in(jax.random.fold_in(rng, 6), position), (parts,), jnp.float32, smallest / len(shards), high / len(shards))
        gain = gain * jnp.repeat(jnp.exp(steps), extent[position] // parts).reshape((-1,) + (1,) * (len(extent) - 1 - position))
    return gain


def noise(key, extent, width, limit, shards=(), dtype=jnp.bfloat16):
    array = width * jax.random.normal(key, extent, jnp.float32)
    if shards:
        array = array * block_levels(key, extent, shards, -0.22, 0.18)
    return jnp.clip(array, -limit, limit).astype(dtype)


def setup_inputs(seed: int = 0) -> dict:
    seeds = jax.random.split(jax.random.key(seed), 6)
    return {
        "queries": noise(seeds[0], (SEQS, TOKENS, HID), HD ** -0.5, 0.5, ((0, 2), (1, 4), (2, 4))),
        "keys": noise(seeds[1], (SEQS, TOKENS, HID), TOKENS ** -0.5, 0.25, ((0, 2), (1, 4), (2, 4))),
        "values": draw_values(jax.random.fold_in(seeds[5], 71), 0),
        "out_gain": jnp.clip(1.0 + 0.18 * jax.random.normal(seeds[3], (HID,), jnp.float32), 0.1, 1.9),
        "grad_out": draw_grad_out(jax.random.fold_in(seeds[5], 71), 0),
    }


EPSILON = 1e-06
MATMUL_PRECISION = lax.Precision.HIGHEST

def split_heads(matrix):
    return matrix.reshape(TOKENS // BLOCK, BLOCK, HEADS, HD).transpose(2, 0, 1, 3)

def join_heads(stacked):
    return stacked.transpose(1, 2, 0, 3).reshape(TOKENS, HID)

def causal_mask():
    return jnp.arange(BLOCK)[:, None] >= jnp.arange(BLOCK)[None, :]

def round_bf16(matrix):
    return lax.optimization_barrier(matrix.astype(jnp.bfloat16)).astype(jnp.float32)

def block_scores(query_matrix_rows, key_rows):
    attention_scores = jnp.einsum('nid,njd->nij', query_matrix_rows, key_rows, precision=MATMUL_PRECISION)
    return round_bf16(jnp.where(causal_mask(), attention_scores, 0.0))

def block_forward(items):
    query_matrix_rows = items[0].astype(jnp.float32)
    key_rows = items[1].astype(jnp.float32)
    value_matrix_rows = items[2].astype(jnp.float32)
    states = jnp.einsum('nbd,nbe->nde', key_rows, value_matrix_rows, precision=MATMUL_PRECISION)
    running = jnp.cumsum(states, axis=0)
    preceding_state_sum = jnp.concatenate([jnp.zeros_like(states[:1]), running[:-1]], axis=0)
    attention_scores = block_scores(query_matrix_rows, key_rows)
    attention_output = jnp.einsum('pqg,pgv->pqv', attention_scores, value_matrix_rows, precision=MATMUL_PRECISION)
    attention_output = attention_output + jnp.einsum('uag,ugl->ual', query_matrix_rows, preceding_state_sum, precision=MATMUL_PRECISION)
    return (attention_output, preceding_state_sum)

def block_backward(items):
    query_matrix_rows = items[0].astype(jnp.float32)
    key_rows = items[1].astype(jnp.float32)
    value_matrix_rows = items[2].astype(jnp.float32)
    upstream_gradient_rows = items[3].astype(jnp.float32)
    preceding_state_sum = items[4]
    block_parts = jnp.einsum('ykw,ykp->ywp', query_matrix_rows, upstream_gradient_rows, precision=MATMUL_PRECISION)
    running = jnp.cumsum(block_parts[::-1], axis=0)[::-1]
    later_sum = jnp.concatenate([running[1:], jnp.zeros_like(block_parts[:1])], axis=0)
    attention_scores = block_scores(query_matrix_rows, key_rows)
    combined_gradient = jnp.einsum('ozy,oly->ozl', upstream_gradient_rows, value_matrix_rows, precision=MATMUL_PRECISION)
    combined_gradient = round_bf16(jnp.where(causal_mask(), combined_gradient, 0.0))
    query_gradient = jnp.einsum('nij,njd->nid', combined_gradient, key_rows, precision=MATMUL_PRECISION)
    query_gradient = query_gradient + jnp.einsum('qbz,qmz->qbm', upstream_gradient_rows, preceding_state_sum, precision=MATMUL_PRECISION)
    grad_keys = jnp.einsum('nij,nid->njd', combined_gradient, query_matrix_rows, precision=MATMUL_PRECISION)
    grad_keys = grad_keys + jnp.einsum('nje,nde->njd', value_matrix_rows, later_sum, precision=MATMUL_PRECISION)
    value_gradient = jnp.einsum('lfa,lfz->laz', attention_scores, upstream_gradient_rows, precision=MATMUL_PRECISION)
    value_gradient = value_gradient + jnp.einsum('njd,nde->nje', key_rows, later_sum, precision=MATMUL_PRECISION)
    return (query_gradient, grad_keys, value_gradient)

def reference(queries, keys, values, out_gain, grad_out):

    def one_sequence(items):
        query_heads = split_heads(items[0])
        key_heads = split_heads(items[1])
        value_heads = split_heads(items[2])
        attention_output, preceding_state_sum = lax.map(block_forward, (query_heads, key_heads, value_heads))
        attention_output = join_heads(attention_output)
        gradient = items[3].astype(jnp.float32)
        rescale = lax.rsqrt(lax.optimization_barrier(jnp.sum(attention_output * attention_output, axis=1, keepdims=True)) / HID + EPSILON)
        normed = (attention_output * rescale * out_gain).astype(jnp.bfloat16)
        gain_part = lax.optimization_barrier(jnp.sum(gradient * attention_output * rescale, axis=0))
        crossed = lax.optimization_barrier(jnp.sum(gradient * out_gain * attention_output, axis=1, keepdims=True))
        upstream = out_gain * gradient * rescale - attention_output * (rescale * rescale * rescale) * crossed / HID
        upstream = lax.optimization_barrier(upstream.astype(jnp.bfloat16))
        grads = lax.map(block_backward, (query_heads, key_heads, value_heads, split_heads(upstream), preceding_state_sum))
        return (normed, join_heads(grads[0]).astype(jnp.bfloat16), join_heads(grads[1]).astype(jnp.bfloat16), join_heads(grads[2]).astype(jnp.bfloat16), gain_part)
    outputs = lax.map(one_sequence, (queries, keys, values, grad_out))
    return (outputs[0], outputs[1], outputs[2], outputs[3], lax.optimization_barrier(jnp.sum(outputs[4], axis=0)))
```

```python
import functools

import jax
import jax.numpy as jnp
from jax import lax
from jax.experimental import pallas as pl
from jax.experimental.pallas import tpu as pltpu
from jax.sharding import PartitionSpec as P

HD = 128
HID = 4096
EPSILON = 1e-06
MESH = pl.DeviceIdType.MESH
F32 = jnp.float32
BF16 = jnp.bfloat16


def dot(a, b, ca, cb):
    return lax.dot_general(a, b, (((ca,), (cb,)), ((), ())), preferred_element_type=F32)


def split(x):
    high = x.astype(BF16)
    return high, (x - high.astype(F32)).astype(BF16)


def dot_wide(a, x, ca, cb):
    high, low = split(x)
    return dot(a, high, ca, cb) + dot(a, low, ca, cb)


def kernel(
    n_seq, n_tp, n_dp,
    q_in, k_in, v_in, gain_in, g_in,
    normed_out, dq_out, dk_out, dv_out, gg_out,
    q_ref, k_ref, v_ref, gain_ref, g_ref,
    prior, total, later, total_back,
    att, scores, up, normed, dq, dk, dv,
    stat, gain_seq, gain_dp, gg,
    in_sem, out_sem,
    up_send, up_recv, down_send, down_recv,
    stat_send, stat_recv, gs_send, gs_recv, gd_send, gd_recv,
):
    rows, width = q_ref.shape
    heads = width // HD
    z = lax.axis_index("seq")
    t = lax.axis_index("tp")
    d = lax.axis_index("dp")
    first, last = z == 0, z == n_seq - 1
    above = lax.rem(z + 1, n_seq)
    below = lax.rem(z + n_seq - 1, n_seq)

    def head(h):
        return slice(h * HD, (h + 1) * HD)

    def peers(axis, me, size):
        return [{axis: lax.rem(me + i, size)} for i in range(1, size)]

    everyone = peers("seq", z, n_seq) + peers("tp", t, n_tp) + peers("dp", d, n_dp)
    barrier = pltpu.get_barrier_semaphore()
    for peer in everyone:
        pl.semaphore_signal(barrier, inc=1, device_id=peer, device_id_type=MESH)

    loads = [
        pltpu.make_async_copy(src, dst, in_sem.at[i])
        for i, (src, dst) in enumerate(
            [(k_in, k_ref), (v_in, v_ref), (q_in, q_ref), (g_in, g_ref), (gain_in, gain_ref)]
        )
    ]
    for load in loads:
        load.start()
    loads[0].wait()
    loads[1].wait()

    def move_up(h):
        return pltpu.make_async_remote_copy(
            src_ref=total.at[h], dst_ref=prior.at[h],
            send_sem=up_send.at[h], recv_sem=up_recv.at[h],
            device_id={"seq": above}, device_id_type=MESH,
        )

    def move_down(h):
        return pltpu.make_async_remote_copy(
            src_ref=total_back.at[h], dst_ref=later.at[h],
            send_sem=down_send.at[h], recv_sem=down_recv.at[h],
            device_id={"seq": below}, device_id_type=MESH,
        )

    for h in range(heads):
        total[h] = dot(k_ref[:, head(h)], v_ref[:, head(h)], 0, 0)
        if h == 0:
            pl.semaphore_wait(barrier, len(everyone))
        if n_seq > 1:
            @pl.when(first)
            def _():
                move_up(h).start()

    @pl.when(first)
    def _():
        prior[...] = jnp.zeros_like(prior)

    @pl.when(last)
    def _():
        later[...] = jnp.zeros_like(later)

    loads[2].wait()
    loads[3].wait()
    loads[4].wait()
    causal = lax.broadcasted_iota(jnp.int32, (rows, rows), 0) >= lax.broadcasted_iota(
        jnp.int32, (rows, rows), 1
    )
    squares = jnp.zeros((rows, HD), F32)
    crossed = jnp.zeros((rows, HD), F32)
    for h in range(heads):
        if n_seq > 1:
            @pl.when(jnp.logical_not(first))
            def _():
                move_up(h).wait_recv()

                @pl.when(jnp.logical_not(last))
                def _():
                    total[h] = total[h] + prior[h]
                    move_up(h).start()

        q = q_ref[:, head(h)]
        v = v_ref[:, head(h)]
        score = jnp.where(causal, dot(q, k_ref[:, head(h)], 1, 1), 0.0).astype(BF16)
        scores[h] = score
        out = dot(score, v, 1, 0) + dot_wide(q, prior[h], 1, 0)
        att[:, head(h)] = out
        squares = squares + out * out
        crossed = crossed + g_ref[:, head(h)].astype(F32) * gain_ref[h:h + 1, :] * out

    stat[t, 0:1, :] = jnp.sum(squares.T, axis=0, keepdims=True)
    stat[t, 1:2, :] = jnp.sum(crossed.T, axis=0, keepdims=True)

    def all_send(buffer, axis, me, size, send, recv):
        return [
            pltpu.make_async_remote_copy(
                src_ref=buffer.at[me], dst_ref=buffer.at[me],
                send_sem=send.at[i - 1], recv_sem=recv.at[i - 1],
                device_id={axis: lax.rem(me + i, size)}, device_id_type=MESH,
            )
            for i in range(1, size)
        ]

    stat_moves = all_send(stat, "tp", t, n_tp, stat_send, stat_recv)
    for move in stat_moves:
        move.start()
    for move in stat_moves:
        move.wait_recv()
    sums = stat[0, 0:2, :]
    for i in range(1, n_tp):
        sums = sums + stat[i, 0:2, :]
    scale_row = lax.rsqrt(sums[0:1] / HID + EPSILON)
    factor_row = scale_row * scale_row * scale_row * sums[1:2] / HID
    scale = jnp.broadcast_to(scale_row, (HD, rows)).T
    factor = jnp.broadcast_to(factor_row, (HD, rows)).T

    def upstream(h):
        out = att[:, head(h)]
        grad = g_ref[:, head(h)].astype(F32)
        scaled = grad * scale
        up[:, head(h)] = (gain_ref[h:h + 1, :] * scaled - out * factor).astype(BF16)
        gain_seq[z, h:h + 1, :] = jnp.sum(scaled * out, axis=0, keepdims=True)

    def back_state(h):
        total_back[h] = dot(q_ref[:, head(h)], up[:, head(h)], 0, 0)
        if n_seq > 1:
            @pl.when(last)
            def _():
                move_down(h).start()

    upstream(0)
    back_state(0)
    for h in range(1, heads):
        upstream(h)
    seq_moves = all_send(gain_seq, "seq", z, n_seq, gs_send, gs_recv)
    for move in seq_moves:
        move.start()
    for h in range(1, heads):
        back_state(h)

    dp_moves = all_send(gain_dp, "dp", d, n_dp, gd_send, gd_recv)
    stores = []

    def store(src, dst):
        copy = pltpu.make_async_copy(src, dst, out_sem.at[len(stores)])
        copy.start()
        stores.append(copy)

    for h in range(heads):
        if n_seq > 1:
            @pl.when(jnp.logical_not(last))
            def _():
                move_down(h).wait_recv()

                @pl.when(jnp.logical_not(first))
                def _():
                    total_back[h] = total_back[h] + later[h]
                    move_down(h).start()

        q, k, v, u = (ref[:, head(h)] for ref in (q_ref, k_ref, v_ref, up))
        normed[:, head(h)] = (att[:, head(h)] * scale * gain_ref[h:h + 1, :]).astype(BF16)
        mixed = jnp.where(causal, dot(u, v, 1, 1), 0.0).astype(BF16)
        dq[:, head(h)] = (dot(mixed, k, 1, 0) + dot_wide(u, prior[h], 1, 1)).astype(BF16)
        high, low = split(later[h])
        dk[:, head(h)] = (
            dot(mixed, q, 0, 0) + dot(v, high, 1, 1) + dot(v, low, 1, 1)
        ).astype(BF16)
        dv[:, head(h)] = (
            dot(scores[h], u, 0, 0) + dot(k, high, 1, 0) + dot(k, low, 1, 0)
        ).astype(BF16)
        for src, dst in ((normed, normed_out), (dq, dq_out), (dk, dk_out), (dv, dv_out)):
            store(src.at[:, head(h)], dst.at[:, head(h)])
        if h == heads // 2:
            for move in seq_moves:
                move.wait_recv()
            gain_sum = gain_seq[0]
            for i in range(1, n_seq):
                gain_sum = gain_sum + gain_seq[i]
            gain_dp[d] = gain_sum
            for move in dp_moves:
                move.start()

    for move in dp_moves:
        move.wait_recv()
    gain_sum = gain_dp[0]
    for i in range(1, n_dp):
        gain_sum = gain_sum + gain_dp[i]
    gg[...] = gain_sum
    store(gg, gg_out)

    for move in stat_moves + seq_moves + dp_moves:
        move.wait_send()
    if n_seq > 1:
        @pl.when(jnp.logical_not(last))
        def _():
            for h in range(heads):
                move_up(h).wait_send()

        @pl.when(jnp.logical_not(first))
        def _():
            for h in range(heads):
                move_down(h).wait_send()
    for copy in stores:
        copy.wait()


def solution(mesh):
    n_seq, n_tp, n_dp = (mesh.shape[name] for name in ("seq", "tp", "dp"))

    def local(queries, keys, values, out_gain, grad_out):
        shape = queries.shape
        rows, width = shape[0] * shape[1], shape[2]
        heads = width // HD
        matrix = jax.ShapeDtypeStruct((rows, width), BF16)
        state = pltpu.VMEM((heads, HD, HD), F32)
        page = pltpu.VMEM((rows, width), BF16)
        sems = pltpu.SemaphoreType.DMA
        flat = lambda x: x.reshape(rows, width)
        outs = pl.pallas_call(
            functools.partial(kernel, n_seq, n_tp, n_dp),
            out_shape=(matrix,) * 4 + (jax.ShapeDtypeStruct((heads, HD), F32),),
            in_specs=[pl.BlockSpec(memory_space=pl.ANY)] * 5,
            out_specs=[pl.BlockSpec(memory_space=pl.ANY)] * 5,
            scratch_shapes=[
                page, page, page, pltpu.VMEM((heads, HD), F32), page,
                state, state, state, state,
                pltpu.VMEM((rows, width), F32),
                pltpu.VMEM((heads, rows, rows), BF16),
                page, page, page, page, page,
                pltpu.VMEM((n_tp, 8, rows), F32),
                pltpu.VMEM((n_seq, heads, HD), F32),
                pltpu.VMEM((n_dp, heads, HD), F32),
                pltpu.VMEM((heads, HD), F32),
                sems((5,)), sems((4 * heads + 1,)),
                sems((heads,)), sems((heads,)), sems((heads,)), sems((heads,)),
                sems((max(n_tp - 1, 1),)), sems((max(n_tp - 1, 1),)),
                sems((max(n_seq - 1, 1),)), sems((max(n_seq - 1, 1),)),
                sems((max(n_dp - 1, 1),)), sems((max(n_dp - 1, 1),)),
            ],
            compiler_params=pltpu.CompilerParams(collective_id=0, has_side_effects=True),
        )(flat(queries), flat(keys), flat(values), out_gain.reshape(heads, HD), flat(grad_out))
        return tuple(x.reshape(shape) for x in outs[:4]) + (outs[4].reshape(width),)

    spec = P("dp", "seq", "tp")
    return jax.shard_map(
        local,
        mesh=mesh,
        in_specs=(spec, spec, spec, P("tp"), spec),
        out_specs=(spec, spec, spec, spec, P("tp")),
        check_vma=False,
    )
```

```python
import functools

import jax
import jax.numpy as jnp
from jax import lax
from jax.experimental import pallas as pl
from jax.experimental.pallas import tpu as pltpu
from jax.sharding import PartitionSpec as P

HD = 128
HID = 4096
EPSILON = 1e-06
PIECES = 4
PART = HD // PIECES
MESH = pl.DeviceIdType.MESH
F32 = jnp.float32
BF16 = jnp.bfloat16


def dot(a, b, ca, cb):
    return lax.dot_general(a, b, (((ca,), (cb,)), ((), ())), preferred_element_type=F32)


def split(x):
    high = x.astype(BF16)
    return high, (x - high.astype(F32)).astype(BF16)


def dot_wide(a, x, ca, cb):
    high, low = split(x)
    return dot(a, high, ca, cb) + dot(a, low, ca, cb)


def kernel(
    n_seq, n_tp, n_dp,
    q_in, k_in, v_in, gain_in, g_in,
    normed_out, dq_out, dk_out, dv_out, gg_out,
    q_ref, k_ref, v_ref, gain_ref, g_ref,
    prior, total, later, total_back,
    att, scores, mixed, squares, crossed, dk_part, dv_part, up, normed, dq, dk, dv,
    stat, gain_seq, gain_dp, gg,
    in_sem, out_sem,
    up_send, up_recv, down_send, down_recv,
    stat_send, stat_recv, gs_send, gs_recv, gd_send, gd_recv,
):
    rows, width = q_ref.shape
    heads = width // HD
    z = lax.axis_index("seq")
    t = lax.axis_index("tp")
    d = lax.axis_index("dp")
    first, last = z == 0, z == n_seq - 1
    above = lax.rem(z + 1, n_seq)
    below = lax.rem(z + n_seq - 1, n_seq)

    def head(h):
        return slice(h * HD, (h + 1) * HD)

    def peers(axis, me, size):
        return [{axis: lax.rem(me + i, size)} for i in range(1, size)]

    everyone = peers("seq", z, n_seq) + peers("tp", t, n_tp) + peers("dp", d, n_dp)
    barrier = pltpu.get_barrier_semaphore()
    for peer in everyone:
        pl.semaphore_signal(barrier, inc=1, device_id=peer, device_id_type=MESH)

    loads = [
        pltpu.make_async_copy(src, dst, in_sem.at[i])
        for i, (src, dst) in enumerate(
            [(k_in, k_ref), (v_in, v_ref), (q_in, q_ref), (g_in, g_ref), (gain_in, gain_ref)]
        )
    ]
    for load in loads:
        load.start()
    loads[0].wait()
    loads[1].wait()

    def part(p):
        return slice(p * PART, (p + 1) * PART)

    def move_up(h, p):
        i = h * PIECES + p
        return pltpu.make_async_remote_copy(
            src_ref=total.at[h, part(p)], dst_ref=prior.at[h, part(p)],
            send_sem=up_send.at[i], recv_sem=up_recv.at[i],
            device_id={"seq": above}, device_id_type=MESH,
        )

    def move_down(h, p):
        i = h * PIECES + p
        return pltpu.make_async_remote_copy(
            src_ref=total_back.at[h, part(p)], dst_ref=later.at[h, part(p)],
            send_sem=down_send.at[i], recv_sem=down_recv.at[i],
            device_id={"seq": below}, device_id_type=MESH,
        )

    def relay(h, p, mine, come, move, is_first, is_last):
        @pl.when(jnp.logical_and(jnp.logical_not(is_first), jnp.logical_not(is_last)))
        def _():
            move(h, p).wait_recv()
            mine[h, part(p)] = mine[h, part(p)] + come[h, part(p)]
            move(h, p).start()

        @pl.when(jnp.logical_and(is_last, jnp.logical_not(is_first)))
        def _():
            move(h, p).wait_recv()

    def relay_all(mine, come, move, is_first, is_last, slots):
        for h in range(heads):
            for p in range(PIECES):
                relay(h, p, mine, come, move, is_first, is_last)
                for step in slots[h * PIECES + p]:
                    step()

    for h in range(heads):
        total[h] = dot(k_ref[:, head(h)], v_ref[:, head(h)], 0, 0)
        if h == 0:
            pl.semaphore_wait(barrier, len(everyone))
        if n_seq > 1:
            @pl.when(first)
            def _():
                for p in range(PIECES):
                    move_up(h, p).start()

    @pl.when(first)
    def _():
        prior[...] = jnp.zeros_like(prior)

    @pl.when(last)
    def _():
        later[...] = jnp.zeros_like(later)

    loads[2].wait()
    loads[3].wait()
    loads[4].wait()
    causal = lax.broadcasted_iota(jnp.int32, (rows, rows), 0) >= lax.broadcasted_iota(
        jnp.int32, (rows, rows), 1
    )
    def score_of(h):
        score = jnp.where(causal, dot(q_ref[:, head(h)], k_ref[:, head(h)], 1, 1), 0.0)
        scores[h] = score.astype(BF16)

    def attend_block(h):
        att[:, head(h)] = dot(scores[h], v_ref[:, head(h)], 1, 0)

    def attend_prior(h):
        att[:, head(h)] = att[:, head(h)] + dot_wide(q_ref[:, head(h)], prior[h], 1, 0)

    def add_stats(h):
        out = att[:, head(h)]
        square = out * out
        cross = g_ref[:, head(h)].astype(F32) * gain_ref[h:h + 1, :] * out
        squares[...] = square if h == 0 else squares[...] + square
        crossed[...] = cross if h == 0 else crossed[...] + cross

    slots = [[] for _ in range(heads * PIECES)]
    for h in range(heads):
        slots[h * PIECES].append(functools.partial(score_of, h))
        slots[h * PIECES + 1].append(functools.partial(attend_block, h))
        if h > 0:
            slots[h * PIECES + 2].append(functools.partial(attend_prior, h - 1))
            slots[h * PIECES + 3].append(functools.partial(add_stats, h - 1))
    relay_all(total, prior, move_up, first, last, slots)
    attend_prior(heads - 1)
    add_stats(heads - 1)

    stat[t, 0:1, :] = jnp.sum(squares[...].T, axis=0, keepdims=True)
    stat[t, 1:2, :] = jnp.sum(crossed[...].T, axis=0, keepdims=True)

    def all_send(buffer, axis, me, size, send, recv):
        return [
            pltpu.make_async_remote_copy(
                src_ref=buffer.at[me], dst_ref=buffer.at[me],
                send_sem=send.at[i - 1], recv_sem=recv.at[i - 1],
                device_id={axis: lax.rem(me + i, size)}, device_id_type=MESH,
            )
            for i in range(1, size)
        ]

    stat_moves = all_send(stat, "tp", t, n_tp, stat_send, stat_recv)
    for move in stat_moves:
        move.start()
    for move in stat_moves:
        move.wait_recv()
    sums = stat[0, 0:2, :]
    for i in range(1, n_tp):
        sums = sums + stat[i, 0:2, :]
    scale_row = lax.rsqrt(sums[0:1] / HID + EPSILON)
    factor_row = scale_row * scale_row * scale_row * sums[1:2] / HID
    scale = jnp.broadcast_to(scale_row, (HD, rows)).T
    factor = jnp.broadcast_to(factor_row, (HD, rows)).T

    def upstream(h):
        out = att[:, head(h)]
        grad = g_ref[:, head(h)].astype(F32)
        scaled = grad * scale
        up[:, head(h)] = (gain_ref[h:h + 1, :] * scaled - out * factor).astype(BF16)
        gain_seq[z, h:h + 1, :] = jnp.sum(scaled * out, axis=0, keepdims=True)

    def back_state(h):
        total_back[h] = dot(q_ref[:, head(h)], up[:, head(h)], 0, 0)
        if n_seq > 1:
            @pl.when(last)
            def _():
                for p in range(PIECES):
                    move_down(h, p).start()

    upstream(0)
    back_state(0)
    for h in range(1, heads):
        upstream(h)
    seq_moves = all_send(gain_seq, "seq", z, n_seq, gs_send, gs_recv)
    for move in seq_moves:
        move.start()
    for h in range(1, heads):
        back_state(h)

    dp_moves = all_send(gain_dp, "dp", d, n_dp, gd_send, gd_recv)
    stores = []

    def store(src, dst):
        copy = pltpu.make_async_copy(src, dst, out_sem.at[len(stores)])
        copy.start()
        stores.append(copy)

    def normed_of(h):
        normed[:, head(h)] = (att[:, head(h)] * scale * gain_ref[h:h + 1, :]).astype(BF16)
        store(normed.at[:, head(h)], normed_out.at[:, head(h)])

    def mixed_of(h):
        mix = jnp.where(causal, dot(up[:, head(h)], v_ref[:, head(h)], 1, 1), 0.0)
        mixed[h] = mix.astype(BF16)

    def dq_of(h):
        dq[:, head(h)] = (
            dot(mixed[h], k_ref[:, head(h)], 1, 0) + dot_wide(up[:, head(h)], prior[h], 1, 1)
        ).astype(BF16)
        store(dq.at[:, head(h)], dq_out.at[:, head(h)])

    def block_parts(h):
        dk_part[h] = dot(mixed[h], q_ref[:, head(h)], 0, 0)
        dv_part[h] = dot(scores[h], up[:, head(h)], 0, 0)

    def dk_of(h):
        wide = dot_wide(v_ref[:, head(h)], later[h], 1, 1)
        dk[:, head(h)] = (dk_part[h] + wide).astype(BF16)
        store(dk.at[:, head(h)], dk_out.at[:, head(h)])

    def dv_of(h):
        wide = dot_wide(k_ref[:, head(h)], later[h], 1, 0)
        dv[:, head(h)] = (dv_part[h] + wide).astype(BF16)
        store(dv.at[:, head(h)], dv_out.at[:, head(h)])

    def gain_middle():
        for move in seq_moves:
            move.wait_recv()
        gain_sum = gain_seq[0]
        for i in range(1, n_seq):
            gain_sum = gain_sum + gain_seq[i]
        gain_dp[d] = gain_sum
        for move in dp_moves:
            move.start()

    block_work = [
        functools.partial(work, h)
        for h in range(heads)
        for work in (mixed_of, dq_of, block_parts, normed_of)
    ]
    half = 2 * heads
    for step in block_work[:half]:
        step()
    slots = [[] for _ in range(heads * PIECES)]
    for h in range(heads):
        if h > 0:
            slots[h * PIECES].append(functools.partial(dk_of, h - 1))
            slots[h * PIECES + 1].append(functools.partial(dv_of, h - 1))
        slots[h * PIECES + 2].append(block_work[half + 2 * h])
        slots[h * PIECES + 3].append(block_work[half + 2 * h + 1])
    slots[(3 * heads // 4) * PIECES].append(gain_middle)
    relay_all(total_back, later, move_down, last, first, slots)
    dk_of(heads - 1)
    dv_of(heads - 1)

    for move in dp_moves:
        move.wait_recv()
    gain_sum = gain_dp[0]
    for i in range(1, n_dp):
        gain_sum = gain_sum + gain_dp[i]
    gg[...] = gain_sum
    store(gg, gg_out)

    for move in stat_moves + seq_moves + dp_moves:
        move.wait_send()
    if n_seq > 1:
        @pl.when(jnp.logical_not(last))
        def _():
            for h in range(heads):
                for p in range(PIECES):
                    move_up(h, p).wait_send()

        @pl.when(jnp.logical_not(first))
        def _():
            for h in range(heads):
                for p in range(PIECES):
                    move_down(h, p).wait_send()
    for copy in stores:
        copy.wait()


def write_out(*refs):
    copies = [pltpu.make_async_copy(refs[i], refs[5 + i], refs[10].at[i]) for i in range(5)]
    for copy in copies:
        copy.start()
    for copy in copies:
        copy.wait()


def solution(mesh):
    n_seq, n_tp, n_dp = (mesh.shape[name] for name in ("seq", "tp", "dp"))

    def local(queries, keys, values, out_gain, grad_out):
        shape = queries.shape
        rows, width = shape[0] * shape[1], shape[2]
        heads = width // HD
        chunks = heads * PIECES
        matrix = jax.ShapeDtypeStruct((rows, width), BF16)
        state = pltpu.VMEM((heads, HD, HD), F32)
        page = pltpu.VMEM((rows, width), BF16)
        sems = pltpu.SemaphoreType.DMA
        flat = lambda x: x.reshape(rows, width)
        outs = pl.pallas_call(
            functools.partial(kernel, n_seq, n_tp, n_dp),
            out_shape=(matrix,) * 4 + (jax.ShapeDtypeStruct((heads, HD), F32),),
            in_specs=[pl.BlockSpec(memory_space=pltpu.HBM)] * 5,
            out_specs=[pl.BlockSpec(memory_space=pl.ANY)] * 5,
            scratch_shapes=[
                page, page, page, pltpu.VMEM((heads, HD), F32), page,
                state, state, state, state,
                pltpu.VMEM((rows, width), F32),
                pltpu.VMEM((heads, rows, rows), BF16), pltpu.VMEM((heads, rows, rows), BF16),
                pltpu.VMEM((rows, HD), F32), pltpu.VMEM((rows, HD), F32),
                pltpu.VMEM((heads, rows, HD), F32), pltpu.VMEM((heads, rows, HD), F32),
                page, page, page, page, page,
                pltpu.VMEM((n_tp, 8, rows), F32),
                pltpu.VMEM((n_seq, heads, HD), F32),
                pltpu.VMEM((n_dp, heads, HD), F32),
                pltpu.VMEM((heads, HD), F32),
                sems((5,)), sems((4 * heads + 1,)),
                sems((chunks,)), sems((chunks,)), sems((chunks,)), sems((chunks,)),
                sems((max(n_tp - 1, 1),)), sems((max(n_tp - 1, 1),)),
                sems((max(n_seq - 1, 1),)), sems((max(n_seq - 1, 1),)),
                sems((max(n_dp - 1, 1),)), sems((max(n_dp - 1, 1),)),
            ],
            compiler_params=pltpu.CompilerParams(collective_id=0, has_side_effects=True, vmem_limit_bytes=32 << 20
            ),
        )(
            *(
                pltpu.with_memory_space_constraint(x, pltpu.HBM)
                for x in (
                    flat(queries), flat(keys), flat(values),
                    out_gain.reshape(heads, HD), flat(grad_out),
                )
            )
        )
        outs = pl.pallas_call(
            write_out,
            out_shape=tuple(jax.ShapeDtypeStruct(x.shape, x.dtype) for x in outs),
            in_specs=[pl.BlockSpec(memory_space=pl.ANY)] * 5,
            out_specs=[pl.BlockSpec(memory_space=pl.ANY)] * 5,
            scratch_shapes=[sems((5,))],
            compiler_params=pltpu.CompilerParams(vmem_limit_bytes=8 << 20),
        )(*outs)
        return tuple(x.reshape(shape) for x in outs[:4]) + (outs[4].reshape(width),)

    spec = P("dp", "seq", "tp")
    return jax.shard_map(
        local,
        mesh=mesh,
        in_specs=(spec, spec, spec, P("tp"), spec),
        out_specs=(spec, spec, spec, spec, P("tp")),
        check_vma=False,
    )
```

```python
import functools

import jax
import jax.numpy as jnp
from jax import lax
from jax.experimental import pallas as pl
from jax.experimental.pallas import tpu as pltpu
from jax.sharding import PartitionSpec as P

HD = 128
HID = 4096
EPSILON = 1e-06
PIECES = 4
PART = HD // PIECES
MESH = pl.DeviceIdType.MESH
F32 = jnp.float32
BF16 = jnp.bfloat16


def dot(a, b, ca, cb):
    return lax.dot_general(a, b, (((ca,), (cb,)), ((), ())), preferred_element_type=F32)


def split(x):
    high = x.astype(BF16)
    return high, (x - high.astype(F32)).astype(BF16)


def dot_wide(a, x, ca, cb):
    high, low = split(x)
    return dot(a, high, ca, cb) + dot(a, low, ca, cb)


def kernel(
    n_seq, n_tp, n_dp,
    q_in, k_in, v_in, gain_in, g_in,
    normed_out, dq_out, dk_out, dv_out, gg_out,
    q_ref, k_ref, v_ref, gain_ref, g_ref,
    prior, total, later, total_back,
    att, scores, mixed, squares, crossed, dk_part, dv_part, up, normed, dq, dk, dv,
    stat, gain_seq, gain_dp, gg, gain_back,
    in_sem, out_sem,
    up_send, up_recv, down_send, down_recv,
    stat_send, stat_recv, gs_send, gs_recv, gd_send, gd_recv,
    gb_send, gb_recv,
):
    rows, width = q_ref.shape
    heads = width // HD
    z = lax.axis_index("seq")
    t = lax.axis_index("tp")
    d = lax.axis_index("dp")
    first, last = z == 0, z == n_seq - 1
    above = lax.rem(z + 1, n_seq)
    below = lax.rem(z + n_seq - 1, n_seq)

    def head(h):
        return slice(h * HD, (h + 1) * HD)

    def peers(axis, me, size):
        return [{axis: lax.rem(me + i, size)} for i in range(1, size)]

    greeted = peers("tp", t, n_tp) + peers("dp", d, n_dp)
    if n_seq > 1:
        greeted.append({"seq": below})
    barrier = pltpu.get_barrier_semaphore()
    for peer in greeted:
        pl.semaphore_signal(barrier, inc=1, device_id=peer, device_id_type=MESH)

    loads = [
        pltpu.make_async_copy(src, dst, in_sem.at[i])
        for i, (src, dst) in enumerate(
            [(k_in, k_ref), (v_in, v_ref), (q_in, q_ref), (g_in, g_ref), (gain_in, gain_ref)]
        )
    ]
    for load in loads:
        load.start()
    loads[0].wait()
    loads[1].wait()

    def part(p):
        return slice(p * PART, (p + 1) * PART)

    def move_up(h, p):
        i = h * PIECES + p
        return pltpu.make_async_remote_copy(
            src_ref=total.at[h, part(p)], dst_ref=prior.at[h, part(p)],
            send_sem=up_send.at[i], recv_sem=up_recv.at[i],
            device_id={"seq": above}, device_id_type=MESH,
        )

    def move_down(h, p):
        i = h * PIECES + p
        return pltpu.make_async_remote_copy(
            src_ref=total_back.at[h, part(p)], dst_ref=later.at[h, part(p)],
            send_sem=down_send.at[i], recv_sem=down_recv.at[i],
            device_id={"seq": below}, device_id_type=MESH,
        )

    def relay(h, p, mine, come, move, is_first, is_last):
        @pl.when(jnp.logical_and(jnp.logical_not(is_first), jnp.logical_not(is_last)))
        def _():
            move(h, p).wait_recv()
            mine[h, part(p)] = mine[h, part(p)] + come[h, part(p)]
            move(h, p).start()

        @pl.when(jnp.logical_and(is_last, jnp.logical_not(is_first)))
        def _():
            move(h, p).wait_recv()

    def relay_all(mine, come, move, is_first, is_last, slots):
        for h in range(heads):
            for p in range(PIECES):
                relay(h, p, mine, come, move, is_first, is_last)
                for step in slots[h * PIECES + p]:
                    step()

    for h in range(heads):
        total[h] = dot(k_ref[:, head(h)], v_ref[:, head(h)], 0, 0)
        if h == 0:
            pl.semaphore_wait(barrier, len(greeted))
        if n_seq > 1:
            @pl.when(first)
            def _():
                for p in range(PIECES):
                    move_up(h, p).start()

    @pl.when(first)
    def _():
        prior[...] = jnp.zeros_like(prior)

    @pl.when(last)
    def _():
        later[...] = jnp.zeros_like(later)

    loads[2].wait()
    loads[3].wait()
    loads[4].wait()
    causal = lax.broadcasted_iota(jnp.int32, (rows, rows), 0) >= lax.broadcasted_iota(
        jnp.int32, (rows, rows), 1
    )
    def score_of(h):
        score = jnp.where(causal, dot(q_ref[:, head(h)], k_ref[:, head(h)], 1, 1), 0.0)
        scores[h] = score.astype(BF16)

    def attend_block(h):
        att[:, head(h)] = dot(scores[h], v_ref[:, head(h)], 1, 0)

    def attend_prior(h):
        att[:, head(h)] = att[:, head(h)] + dot_wide(q_ref[:, head(h)], prior[h], 1, 0)

    def add_stats(h):
        out = att[:, head(h)]
        square = out * out
        cross = g_ref[:, head(h)].astype(F32) * gain_ref[h:h + 1, :] * out
        squares[...] = square if h == 0 else squares[...] + square
        crossed[...] = cross if h == 0 else crossed[...] + cross

    slots = [[] for _ in range(heads * PIECES)]
    for h in range(heads):
        slots[h * PIECES].append(functools.partial(score_of, h))
        slots[h * PIECES + 1].append(functools.partial(attend_block, h))
        if h > 0:
            slots[h * PIECES + 2].append(functools.partial(attend_prior, h - 1))
            slots[h * PIECES + 3].append(functools.partial(add_stats, h - 1))
    relay_all(total, prior, move_up, first, last, slots)
    attend_prior(heads - 1)
    add_stats(heads - 1)

    stat[t, 0:1, :] = jnp.sum(squares[...].T, axis=0, keepdims=True)
    stat[t, 1:2, :] = jnp.sum(crossed[...].T, axis=0, keepdims=True)

    def all_send(buffer, axis, me, size, send, recv):
        return [
            pltpu.make_async_remote_copy(
                src_ref=buffer.at[me], dst_ref=buffer.at[me],
                send_sem=send.at[i - 1], recv_sem=recv.at[i - 1],
                device_id={axis: lax.rem(me + i, size)}, device_id_type=MESH,
            )
            for i in range(1, size)
        ]

    stat_moves = all_send(stat, "tp", t, n_tp, stat_send, stat_recv)
    for move in stat_moves:
        move.start()
    for move in stat_moves:
        move.wait_recv()
    sums = stat[0, 0:2, :]
    for i in range(1, n_tp):
        sums = sums + stat[i, 0:2, :]
    scale_row = lax.rsqrt(sums[0:1] / HID + EPSILON)
    factor_row = scale_row * scale_row * scale_row * sums[1:2] / HID
    scale = jnp.broadcast_to(scale_row, (HD, rows)).T
    factor = jnp.broadcast_to(factor_row, (HD, rows)).T

    def upstream(h):
        out = att[:, head(h)]
        grad = g_ref[:, head(h)].astype(F32)
        scaled = grad * scale
        up[:, head(h)] = (gain_ref[h:h + 1, :] * scaled - out * factor).astype(BF16)
        gain_seq[z, h:h + 1, :] = jnp.sum(scaled * out, axis=0, keepdims=True)

    def back_state(h):
        total_back[h] = dot(q_ref[:, head(h)], up[:, head(h)], 0, 0)
        if n_seq > 1:
            @pl.when(last)
            def _():
                for p in range(PIECES):
                    move_down(h, p).start()

    upstream(0)
    back_state(0)
    for h in range(1, heads):
        upstream(h)

    def gain_to_first(source):
        return pltpu.make_async_remote_copy(
            src_ref=gain_seq.at[source], dst_ref=gain_seq.at[source],
            send_sem=gs_send.at[source], recv_sem=gs_recv.at[source],
            device_id={"seq": 0}, device_id_type=MESH,
        )

    def gain_from_first(target):
        return pltpu.make_async_remote_copy(
            src_ref=gg, dst_ref=gain_back,
            send_sem=gb_send.at[target], recv_sem=gb_recv.at[target],
            device_id={"seq": target}, device_id_type=MESH,
        )

    @pl.when(jnp.logical_not(first))
    def _():
        gain_to_first(z).start()

    for h in range(1, heads):
        back_state(h)

    dp_moves = all_send(gain_dp, "dp", d, n_dp, gd_send, gd_recv)
    stores = []

    def store(src, dst):
        copy = pltpu.make_async_copy(src, dst, out_sem.at[len(stores)])
        copy.start()
        stores.append(copy)

    def normed_of(h):
        normed[:, head(h)] = (att[:, head(h)] * scale * gain_ref[h:h + 1, :]).astype(BF16)
        store(normed.at[:, head(h)], normed_out.at[:, head(h)])

    def mixed_of(h):
        mix = jnp.where(causal, dot(up[:, head(h)], v_ref[:, head(h)], 1, 1), 0.0)
        mixed[h] = mix.astype(BF16)

    def dq_of(h):
        dq[:, head(h)] = (
            dot(mixed[h], k_ref[:, head(h)], 1, 0) + dot_wide(up[:, head(h)], prior[h], 1, 1)
        ).astype(BF16)
        store(dq.at[:, head(h)], dq_out.at[:, head(h)])

    def block_parts(h):
        dk_part[h] = dot(mixed[h], q_ref[:, head(h)], 0, 0)
        dv_part[h] = dot(scores[h], up[:, head(h)], 0, 0)

    def dk_of(h):
        wide = dot_wide(v_ref[:, head(h)], later[h], 1, 1)
        dk[:, head(h)] = (dk_part[h] + wide).astype(BF16)
        store(dk.at[:, head(h)], dk_out.at[:, head(h)])

    def dv_of(h):
        wide = dot_wide(k_ref[:, head(h)], later[h], 1, 0)
        dv[:, head(h)] = (dv_part[h] + wide).astype(BF16)
        store(dv.at[:, head(h)], dv_out.at[:, head(h)])

    def gain_middle():
        @pl.when(first)
        def _():
            for source in range(1, n_seq):
                gain_to_first(source).wait_recv()
            gain_sum = gain_seq[0]
            for i in range(1, n_seq):
                gain_sum = gain_sum + gain_seq[i]
            gain_dp[d] = gain_sum
            for move in dp_moves:
                move.start()

    def gain_end():
        @pl.when(first)
        def _():
            for move in dp_moves:
                move.wait_recv()
            gain_sum = gain_dp[0]
            for i in range(1, n_dp):
                gain_sum = gain_sum + gain_dp[i]
            gg[...] = gain_sum
            for target in range(1, n_seq):
                gain_from_first(target).start()

    block_work = [
        functools.partial(work, h)
        for h in range(heads)
        for work in (mixed_of, dq_of, block_parts, normed_of)
    ]
    half = 2 * heads
    for step in block_work[:half]:
        step()
    slots = [[] for _ in range(heads * PIECES)]
    for h in range(heads):
        if h > 0:
            slots[h * PIECES].append(functools.partial(dk_of, h - 1))
            slots[h * PIECES + 1].append(functools.partial(dv_of, h - 1))
        slots[h * PIECES + 2].append(block_work[half + 2 * h])
        slots[h * PIECES + 3].append(block_work[half + 2 * h + 1])
    slots[0].append(gain_middle)
    slots[heads // 4 * PIECES].append(gain_end)
    relay_all(total_back, later, move_down, last, first, slots)
    dk_of(heads - 1)
    dv_of(heads - 1)

    gg_copy = pltpu.make_async_copy(gg, gg_out, out_sem.at[4 * heads])

    @pl.when(first)
    def _():
        gg_copy.start()
        for move in dp_moves:
            move.wait_send()
        for target in range(1, n_seq):
            gain_from_first(target).wait_send()

    back_copy = pltpu.make_async_copy(gain_back, gg_out, out_sem.at[4 * heads])

    @pl.when(jnp.logical_not(first))
    def _():
        gain_from_first(z).wait_recv()
        back_copy.start()
        gain_to_first(z).wait_send()

    for move in stat_moves:
        move.wait_send()
    if n_seq > 1:
        @pl.when(jnp.logical_not(last))
        def _():
            for h in range(heads):
                for p in range(PIECES):
                    move_up(h, p).wait_send()

        @pl.when(jnp.logical_not(first))
        def _():
            for h in range(heads):
                for p in range(PIECES):
                    move_down(h, p).wait_send()
    for copy in stores:
        copy.wait()

    @pl.when(first)
    def _():
        gg_copy.wait()

    @pl.when(jnp.logical_not(first))
    def _():
        back_copy.wait()


def write_out(*refs):
    copies = [pltpu.make_async_copy(refs[i], refs[5 + i], refs[10].at[i]) for i in range(5)]
    for copy in copies:
        copy.start()
    for copy in copies:
        copy.wait()


def solution(mesh):
    n_seq, n_tp, n_dp = (mesh.shape[name] for name in ("seq", "tp", "dp"))

    def local(queries, keys, values, out_gain, grad_out):
        shape = queries.shape
        rows, width = shape[0] * shape[1], shape[2]
        heads = width // HD
        chunks = heads * PIECES
        matrix = jax.ShapeDtypeStruct((rows, width), BF16)
        state = pltpu.VMEM((heads, HD, HD), F32)
        page = pltpu.VMEM((rows, width), BF16)
        sems = pltpu.SemaphoreType.DMA
        flat = lambda x: x.reshape(rows, width)
        outs = pl.pallas_call(
            functools.partial(kernel, n_seq, n_tp, n_dp),
            out_shape=(matrix,) * 4 + (jax.ShapeDtypeStruct((heads, HD), F32),),
            in_specs=[pl.BlockSpec(memory_space=pltpu.HBM)] * 5,
            out_specs=[pl.BlockSpec(memory_space=pl.ANY)] * 5,
            scratch_shapes=[
                page, page, page, pltpu.VMEM((heads, HD), F32), page,
                state, state, state, state,
                pltpu.VMEM((rows, width), F32),
                pltpu.VMEM((heads, rows, rows), BF16), pltpu.VMEM((heads, rows, rows), BF16),
                pltpu.VMEM((rows, HD), F32), pltpu.VMEM((rows, HD), F32),
                pltpu.VMEM((heads, rows, HD), F32), pltpu.VMEM((heads, rows, HD), F32),
                page, page, page, page, page,
                pltpu.VMEM((n_tp, 8, rows), F32),
                pltpu.VMEM((n_seq, heads, HD), F32),
                pltpu.VMEM((n_dp, heads, HD), F32),
                pltpu.VMEM((heads, HD), F32), pltpu.VMEM((heads, HD), F32),
                sems((5,)), sems((4 * heads + 1,)),
                sems((chunks,)), sems((chunks,)), sems((chunks,)), sems((chunks,)),
                sems((max(n_tp - 1, 1),)), sems((max(n_tp - 1, 1),)),
                sems((n_seq,)), sems((n_seq,)),
                sems((max(n_dp - 1, 1),)), sems((max(n_dp - 1, 1),)),
                sems((n_seq,)), sems((n_seq,)),
            ],
            compiler_params=pltpu.CompilerParams(collective_id=0, has_side_effects=True, vmem_limit_bytes=32 << 20
            ),
        )(
            *(
                pltpu.with_memory_space_constraint(x, pltpu.HBM)
                for x in (
                    flat(queries), flat(keys), flat(values),
                    out_gain.reshape(heads, HD), flat(grad_out),
                )
            )
        )
        outs = pl.pallas_call(
            write_out,
            out_shape=tuple(jax.ShapeDtypeStruct(x.shape, x.dtype) for x in outs),
            in_specs=[pl.BlockSpec(memory_space=pl.ANY)] * 5,
            out_specs=[pl.BlockSpec(memory_space=pl.ANY)] * 5,
            scratch_shapes=[sems((5,))],
            compiler_params=pltpu.CompilerParams(vmem_limit_bytes=8 << 20),
        )(*outs)
        return tuple(x.reshape(shape) for x in outs[:4]) + (outs[4].reshape(width),)

    spec = P("dp", "seq", "tp")
    return jax.shard_map(
        local,
        mesh=mesh,
        in_specs=(spec, spec, spec, P("tp"), spec),
        out_specs=(spec, spec, spec, spec, P("tp")),
        check_vma=False,
    )
```
